32 devices in a mesh: attn: 4 (over y, core), expert: 4 (over z), loop: 2 (over x).
Axes of the slice: x: 2, y: 2, z: 4, core: 2. Of those that a mesh axis runs over, the one named last changes fastest.
Arguments:
- resid: bfloat16 [64, 3072], P(('expert', 'loop', 'attn')), may hold values from -33 to 33
- query: bfloat16 [64, 3072], P(('expert', 'loop', 'attn')), may hold values from -68.75573 to 68.75573
- key_cache: bfloat16 [64, 256, 512], P(('expert', 'loop', 'attn')), may hold values from -6 to 6
- value_cache: bfloat16 [64, 256, 512], P(('expert', 'loop', 'attn')), may hold values from -6 to 6
- new_key: bfloat16 [64, 512], P(('expert', 'loop', 'attn')), may hold values from -6 to 6
- new_value: bfloat16 [64, 512], P(('expert', 'loop', 'attn')), may hold values from -6 to 6
- cache_len: int32 [64], P(('expert', 'loop', 'attn')), may hold values from 2 to 256, as said below
- norm_gain: float32 [3072], replicated, may hold values from 0.5 to 1.5
- gate_weight: bfloat16 [4, 3072, 8192], P('expert', 'attn', 'loop'), may hold values from -0.109375 to 0.109375
- up_weight: bfloat16 [4, 3072, 8192], P('expert', 'attn', 'loop'), may hold values from -0.109375 to 0.109375
- down_weight: bfloat16 [4, 8192, 3072], P('expert', 'loop', 'attn'), may hold values from -0.0625 to 0.0625
- block_rows: int32 [4, 1, 128], P('expert'), may hold values from -1 to 63, as said below
- slot_weight: float32 [4, 1, 128], P('expert'), may hold values from 0.1 to 1
Outputs:
- layer_out: bfloat16 [64, 3072], P(('expert', 'loop', 'attn'))
The draws below stay inside these ranges and needn't reach their ends.
Inputs may be any that keep to these rules, and one draw needn't show every extreme that they name: `block_rows`: each of the 64 rows is named in the lists of exactly two different experts and nowhere else; within a list the rows ascend and fill the slots from the first one on; unused slots hold -1. One expert, drawn from the seed, is named by exactly 32 rows; the other experts by nearly equal numbers of rows. `cache_len`: some row uses all 256 positions.
All inputs are finite; a program needn't handle non-finite values.
Results may differ from the reference program's by a relative error of at most 0.0054.
Values may be sent and summed in bfloat16 or wider, within the bound.
A program may use at most 128 MiB of HBM per device.

```python
import math
import jax
import jax.numpy as jnp
from jax import lax

D = 3072
Q_HEADS = 24
KV_HEADS = 4
HEAD = 128
FF = 8192
BLOCK = 128
CACHE = 256
EXPERTS = 4
ROWS = 64
HOT = 32
CAP_BLOCKS = 1


def attention_keys(key):
    base_key = jax.random.fold_in(key, 23)
    key_main, key_query = jax.random.split(base_key)
    shape = (ROWS, CACHE, KV_HEADS * HEAD)
    cached = jnp.clip(jax.random.normal(key_main, shape, jnp.float32), -6.0, 6.0)
    return (cached, key_query)


def draw_key_cache(key, part):
    cached, key_query = attention_keys(key)
    return cached.astype(jnp.bfloat16)


def draw_query(key, part):
    cached, key_query = attention_keys(key)
    shape = (ROWS, Q_HEADS * HEAD)
    drawn = jnp.clip(jax.random.normal(key_query, shape, jnp.float32), -6.0, 6.0)
    return drawn.astype(jnp.bfloat16)


def draw_resid(key, part):
    base_key = jax.random.fold_in(key, 5)
    key_base, key_rows = jax.random.split(base_key, 2)
    row_scale = jnp.exp(jax.random.uniform(key_rows, (ROWS, 1), jnp.float32, math.log(0.32), math.log(3.2)))
    values = jnp.clip(jax.random.normal(key_base, (ROWS, D), jnp.float32), -6.0, 6.0) * row_scale
    return values.astype(jnp.bfloat16)


def draw_cache_len(key, part):
    lengths = jax.random.randint(jax.random.fold_in(key, 31), (ROWS,), 2, CACHE + 1)
    return lengths.at[0].set(CACHE).astype(jnp.int32)


def draw_block_rows(key, part):
    routing_key = jax.random.fold_in(key, 7)
    key_expert, key_row = jax.random.split(routing_key)
    expert_order = jax.random.permutation(key_expert, EXPERTS).astype(jnp.int32)
    hot_expert = expert_order[0]
    cold_experts = expert_order[1:]
    others = EXPERTS - 1
    row_order = jax.random.permutation(key_row, ROWS).astype(jnp.int32)
    position = jnp.arange(ROWS, dtype=jnp.int32)
    cold_place = jnp.maximum(position - HOT, 0)
    first_choice = jnp.where(position < HOT, hot_expert, cold_experts[cold_place % others])
    second_hot = cold_experts[position % others]
    second_cold = cold_experts[(cold_place + 1 + cold_place // others % (others - 1)) % others]
    second_choice = jnp.where(position < HOT, second_hot, second_cold)
    first_row = jnp.zeros((ROWS,), jnp.int32).at[row_order].set(first_choice)
    second_row = jnp.zeros((ROWS,), jnp.int32).at[row_order].set(second_choice)
    expert_ids = jnp.arange(EXPERTS, dtype=jnp.int32)[None, :]
    member = (first_row[:, None] == expert_ids) | (second_row[:, None] == expert_ids)
    member_count = member.astype(jnp.int32)
    list_rank = jnp.cumsum(member_count, axis=0) - 1
    list_slot = jnp.where(member, list_rank, CAP_BLOCKS * BLOCK)
    row_ids = jnp.broadcast_to(jnp.arange(ROWS, dtype=jnp.int32)[:, None], (ROWS, EXPERTS))
    column_ids = jnp.broadcast_to(expert_ids, (ROWS, EXPERTS))
    list_table = jnp.full((EXPERTS, CAP_BLOCKS * BLOCK), -1, jnp.int32)
    list_table = list_table.at[column_ids, list_slot].set(row_ids, mode='drop')
    return list_table.reshape(EXPERTS, CAP_BLOCKS, BLOCK)


def levels(rng, dims, shards, smallest, high):
    def one(dim, shards_of):
        heights = jax.random.uniform(jax.random.fold_in(jax.random.fold_in(rng, 6), dim), (shards_of,), jnp.float32, smallest / len(shards), high / len(shards))
        return jnp.repeat(jnp.exp(heights), dims[dim] // shards_of).reshape((-1,) + (1,) * (len(dims) - dim - 1))

    loudness = one(*shards[0])
    for cut in shards[1:]:
        loudness = loudness * one(*cut)
    return loudness


def gaussian(stream_key, dims, spread, most, pieces=(), kind=jnp.bfloat16):
    gain = levels(stream_key, dims, pieces, -0.22, 0.18) if pieces else 1.0
    drawn = jax.random.normal(stream_key, dims, jnp.float32) * spread * gain
    return jnp.minimum(jnp.maximum(drawn, -most), most).astype(kind)


def setup_inputs(seed: int = 0) -> dict:
    splits = jax.random.split(jax.random.key(seed), 14)
    resid = draw_resid(jax.random.fold_in(splits[13], 71), 0)
    query = draw_query(jax.random.fold_in(splits[13], 71), 0)
    key_cache = draw_key_cache(jax.random.fold_in(splits[13], 71), 0)
    value_cache = gaussian(splits[3], (ROWS, CACHE, KV_HEADS * HEAD), 1.0, 6.0, ((0, 32),))
    new_key = gaussian(splits[4], (ROWS, KV_HEADS * HEAD), 1.0, 6.0, ((0, 32),))
    new_value = gaussian(splits[5], (ROWS, KV_HEADS * HEAD), 1.0, 6.0, ((0, 32),))
    cache_len = draw_cache_len(jax.random.fold_in(splits[13], 71), 0)
    norm_gain = jnp.clip(jax.random.uniform(splits[7], (D,), jnp.float32, 0.5, 1.5), 0.5, 1.5)
    gate_weight = gaussian(splits[8], (EXPERTS, D, FF), D ** -0.5, 0.109375, ((0, 4), (1, 4), (2, 2)))
    up_weight = gaussian(splits[9], (EXPERTS, D, FF), D ** -0.5, 0.109375, ((0, 4), (1, 4), (2, 2)))
    down_weight = gaussian(splits[10], (EXPERTS, FF, D), FF ** -0.5, 0.0625, ((0, 4), (1, 2), (2, 4)))
    block_rows = draw_block_rows(jax.random.fold_in(splits[13], 71), 0)
    slot_weight = jnp.clip(0.1 + 0.9 * jax.random.uniform(splits[12], (EXPERTS, CAP_BLOCKS, BLOCK), jnp.float32) ** levels(splits[12], (EXPERTS, CAP_BLOCKS, BLOCK), ((0, 4),), -0.2, 0.2), 0.1, 1.0)
    return {"resid": resid, "query": query, "key_cache": key_cache, "value_cache": value_cache, "new_key": new_key, "new_value": new_value, "cache_len": cache_len, "norm_gain": norm_gain, "gate_weight": gate_weight, "up_weight": up_weight, "down_weight": down_weight, "block_rows": block_rows, "slot_weight": slot_weight}


def reference(resid, query, key_cache, value_cache, new_key, new_value, cache_len, norm_gain, gate_weight, up_weight, down_weight, block_rows, slot_weight):
    groups = Q_HEADS // KV_HEADS
    score_scale = HEAD ** (-0.5)
    highest = lax.Precision.HIGHEST

    def one_row(row_item):
        q_row, k_row, v_row, k_new, v_new, length = row_item
        queries = q_row.astype(jnp.float32).reshape(KV_HEADS, groups, HEAD)
        all_keys = jnp.concatenate([k_row, k_new[None, :]], axis=0).astype(jnp.float32).reshape(CACHE + 1, KV_HEADS, HEAD)
        all_values = jnp.concatenate([v_row, v_new[None, :]], axis=0).astype(jnp.float32).reshape(CACHE + 1, KV_HEADS, HEAD)
        scores = jnp.einsum('kgd,lkd->kgl', queries, all_keys, precision=highest) * score_scale
        position = jnp.arange(CACHE + 1)
        cache_live = (position < length) | (position == CACHE)
        scores = jnp.where(cache_live[None, None, :], scores, -jnp.inf)
        row_max = lax.optimization_barrier(jnp.max(scores, axis=-1, keepdims=True))
        exponent = jnp.exp(scores - row_max)
        softmax_weights = (exponent / lax.optimization_barrier(jnp.sum(exponent, axis=-1, keepdims=True))).astype(jnp.bfloat16)
        softmax_weights = lax.optimization_barrier(softmax_weights).astype(jnp.float32)
        attended = jnp.einsum('kgl,lkd->kgd', softmax_weights, all_values, precision=highest)
        return attended.reshape(Q_HEADS * HEAD)
    attended = lax.map(one_row, (query, key_cache, value_cache, new_key, new_value, cache_len))
    residual = (resid.astype(jnp.float32) + attended).astype(jnp.bfloat16)
    residual_wide = residual.astype(jnp.float32)
    normed = (residual_wide * lax.rsqrt(lax.optimization_barrier(jnp.mean(residual_wide * residual_wide, axis=-1, keepdims=True)) + 1e-05) * norm_gain).astype(jnp.bfloat16)
    slot_total = CAP_BLOCKS * BLOCK

    def one_expert(accumulated, expert_item):
        list_rows, weights, w_gate, w_up, w_down = expert_item
        slot_rows = list_rows.reshape(slot_total)
        slot_live = slot_rows >= 0
        picked = jnp.take(normed, jnp.where(slot_live, slot_rows, 0), axis=0)
        picked = jnp.where(slot_live[:, None], picked, jnp.zeros_like(picked))
        gate_total = jnp.dot(picked, w_gate, preferred_element_type=jnp.float32)
        up_total = jnp.dot(picked, w_up, preferred_element_type=jnp.float32)
        hidden = (jax.nn.silu(gate_total) * up_total).astype(jnp.bfloat16)
        expert_out = jnp.dot(hidden, w_down, preferred_element_type=jnp.float32)
        weighted = expert_out * jnp.where(slot_live, weights.reshape(slot_total), 0.0)[:, None]
        target = jnp.where(slot_live, slot_rows, ROWS)
        return (accumulated.at[target].add(weighted, mode='drop'), None)
    mixture, _ = lax.scan(one_expert, jnp.zeros((ROWS, D), jnp.float32), (block_rows, slot_weight, gate_weight, up_weight, down_weight))
    moe = lax.optimization_barrier(mixture.astype(jnp.bfloat16))
    return (residual.astype(jnp.float32) + moe.astype(jnp.float32)).astype(jnp.bfloat16)
```

```python
import functools

import jax
import jax.numpy as jnp
from jax import lax
from jax.experimental import pallas as pl
from jax.experimental.pallas import tpu as pltpu
from jax.sharding import PartitionSpec as P

Q_HEADS = 24
KV_HEADS = 4
HEAD = 128
MESH = pl.DeviceIdType.MESH
F32 = jnp.float32
BF16 = jnp.bfloat16
CUTS = 2
VMEM_LIMIT = 56 << 20


def kernel(
    sizes,
    len_hbm,
    resid_hbm,
    query_hbm,
    nk_hbm,
    nv_hbm,
    gain_hbm,
    list_hbm,
    slotw_hbm,
    kc_hbm,
    vc_hbm,
    wg_hbm,
    wu_hbm,
    wd_hbm,
    out_ref,
    len_ref,
    resid_ref,
    query_ref,
    nk_ref,
    nv_ref,
    gain_ref,
    list_ref,
    slotw_ref,
    in_sem,
    kc,
    vc,
    wg,
    wu,
    wd,
    nb,
    xr,
    x32,
    ps,
    pr,
    own,
    cs,
    cr,
    hid,
    d32,
    ys,
    yr,
    kv_sem,
    w_sem,
    d_sem,
    x_send,
    x_recv,
    p_send,
    p_recv,
    c_send,
    c_recv,
    h_send,
    h_recv,
    f_send,
    f_recv,
    y_send,
    y_recv,
):
    n, experts, loops, cap, cuts = sizes
    total = n * experts * loops
    chips = n // 2
    here, width = resid_ref.shape
    cache = kc.shape[1]
    part = width // n
    piece = wg.shape[2]
    quarter = piece * cuts
    rows = total * here
    slots = list_ref.shape[1]
    me_a = lax.axis_index("attn")
    me_e = lax.axis_index("expert")
    me_l = lax.axis_index("loop")
    me = (me_e * loops + me_l) * n + me_a
    core = lax.rem(me_a, 2)
    chip = lax.div(me_a, 2)
    partner = {"attn": chip * 2 + 1 - core, "expert": me_e, "loop": me_l}

    sources = total // n
    group = me_e * loops + me_l
    lanes_of = [lax.rem(me_a + d, n) for d in range(n)]

    def peers_of(d, first, act):
        other = group ^ d if sources & (sources - 1) == 0 else lax.rem(group + d, sources)
        expert = lax.div(other, loops)
        loop = lax.rem(other, loops)
        for k in range(first, n):
            act(
                other * n + lanes_of[k],
                lanes_of[k],
                {"attn": lanes_of[k], "expert": expert, "loop": loop},
            )

    def each_peer(act):
        def step(d, carry):
            peers_of(sources - d, 0, act)
            return carry

        lax.fori_loop(1, sources, step, 0, unroll=sources <= 8)
        peers_of(0, 1, act)

    def side_of(shift, side):
        at = lax.rem(chip + shift + chips, chips)
        return at * 2 + (core if side else 1 - core)

    barrier = pltpu.get_barrier_semaphore()

    def greet(index, lane, device):
        pl.semaphore_signal(barrier, inc=1, device_id=device, device_id_type=MESH)

    in_copies = [
        pltpu.make_async_copy(source, target, in_sem.at[k])
        for k, (source, target) in enumerate(
            (
                (query_hbm, query_ref),
                (nk_hbm, nk_ref),
                (nv_hbm, nv_ref),
                (len_hbm, len_ref),
                (resid_hbm, resid_ref),
                (gain_hbm, gain_ref),
                (list_hbm, list_ref),
                (slotw_hbm, slotw_ref),
            )
        )
    ]
    k_copies = [pltpu.make_async_copy(kc_hbm.at[r], kc.at[r], kv_sem.at[0, r]) for r in range(here)]
    v_copies = [pltpu.make_async_copy(vc_hbm.at[r], vc.at[r], kv_sem.at[1, r]) for r in range(here)]
    for copy in in_copies[:4] + k_copies + in_copies[4:] + v_copies:
        copy.start()
    each_peer(greet)

    shifts = list(range(1, chips)) + [0]
    w_copies = {}
    for shift in shifts:
        for side in range(2):
            for cut in range(cuts):
                k = len(w_copies)
                col = pl.multiple_of(side_of(shift, side) * quarter + cut * piece, piece)
                pair = (
                    pltpu.make_async_copy(
                        wg_hbm.at[0, :, pl.ds(col, piece)], wg.at[k], w_sem.at[0, k]
                    ),
                    pltpu.make_async_copy(
                        wu_hbm.at[0, :, pl.ds(col, piece)], wu.at[k], w_sem.at[1, k]
                    ),
                )
                for copy in pair:
                    copy.start()
                w_copies[shift, side, cut] = (k, pair)
    d_copies = []
    for shift in range(chips):
        for j in range(2):
            for cut in range(cuts):
                k = (2 * shift + j) * cuts + cut
                row = pl.multiple_of(side_of(-shift, 1 - j) * quarter + cut * piece, piece)
                copy = pltpu.make_async_copy(
                    wd_hbm.at[0, pl.ds(row, piece), :], wd.at[k], d_sem.at[k]
                )
                copy.start()
                d_copies.append(copy)

    groups = Q_HEADS // KV_HEADS
    scale = HEAD ** (-0.5)
    heads = here * Q_HEADS
    for copy in in_copies:
        copy.wait()
    head_of = lax.rem(lax.broadcasted_iota(jnp.int32, (heads, HEAD), 0), Q_HEADS) // groups
    row_of = lax.broadcasted_iota(jnp.int32, (heads, cache), 0) // Q_HEADS
    position = lax.broadcasted_iota(jnp.int32, (heads, cache), 1)
    live = len_ref[0]
    for r in range(1, here):
        live = jnp.where(row_of >= r, len_ref[r], live)
    queries = query_ref[...].astype(F32)
    new_keys = nk_ref[...].astype(F32)
    new_values = nv_ref[...].astype(F32)
    q_all = jnp.concatenate(
        [
            queries[r : r + 1, j * HEAD : (j + 1) * HEAD]
            for r in range(here)
            for j in range(Q_HEADS)
        ],
        axis=0,
    )

    def own_rows(new):
        return jnp.concatenate(
            [
                jnp.broadcast_to(new[r : r + 1, g * HEAD : (g + 1) * HEAD], (groups, HEAD))
                for r in range(here)
                for g in range(KV_HEADS)
            ],
            axis=0,
        )

    own_key, own_value = own_rows(new_keys), own_rows(new_values)
    q_wide = jnp.concatenate(
        [jnp.where(head_of == g, q_all, 0.0) for g in range(KV_HEADS)], axis=1
    ).astype(BF16)
    own_score = jnp.sum(q_all * own_key, axis=1, keepdims=True) * scale

    rows_pad = max(rows, 128)
    slot_rows = list_ref[...]
    hot_t = jnp.where(
        lax.broadcasted_iota(jnp.int32, (rows_pad, slots), 0) == slot_rows, 1.0, 0.0
    ).astype(F32)
    hot = hot_t.T[:cap, :rows].astype(BF16)
    hot_t = hot_t[:rows]
    row_weight = jnp.sum(hot_t * slotw_ref[...], axis=1, keepdims=True)
    hot_t = hot_t.astype(BF16)

    for copy in k_copies:
        copy.wait()
    scores = jnp.concatenate(
        [
            lax.dot_general(
                q_wide[r * Q_HEADS : (r + 1) * Q_HEADS],
                kc[r],
                (((1,), (1,)), ((), ())),
                preferred_element_type=F32,
            )
            for r in range(here)
        ],
        axis=0,
    )
    scores = jnp.where(position < live, scores * scale, -jnp.inf)
    top = jnp.maximum(jnp.max(scores, axis=1, keepdims=True), own_score)
    exps = jnp.exp(scores - top)
    own_exp = jnp.exp(own_score - top)
    denominator = jnp.sum(exps, axis=1, keepdims=True) + own_exp
    probs = (exps / denominator).astype(BF16)
    own_prob = (own_exp / denominator).astype(BF16).astype(F32)
    for copy in v_copies:
        copy.wait()
    mixed = jnp.concatenate(
        [
            jnp.dot(
                probs[r * Q_HEADS : (r + 1) * Q_HEADS], vc[r], preferred_element_type=F32
            )
            for r in range(here)
        ],
        axis=0,
    )
    attended = own_prob * own_value
    for g in range(KV_HEADS):
        attended = attended + jnp.where(
            head_of == g, mixed[:, g * HEAD : (g + 1) * HEAD], 0.0
        )
    attended = jnp.concatenate(
        [
            jnp.concatenate(
                [attended[r * Q_HEADS + j : r * Q_HEADS + j + 1, :] for j in range(Q_HEADS)],
                axis=1,
            )
            for r in range(here)
        ],
        axis=0,
    )
    residual = (resid_ref[...].astype(F32) + attended).astype(BF16).astype(F32)
    normed = (
        residual
        * lax.rsqrt(jnp.mean(residual * residual, axis=-1, keepdims=True) + 1e-05)
        * gain_ref[...]
    ).astype(BF16)
    for a in range(n):
        nb[a] = normed[:, a * part : (a + 1) * part]

    pl.semaphore_wait(barrier, total - 1)

    def send_x(index, lane, device):
        pltpu.make_async_remote_copy(
            src_ref=nb.at[lane],
            dst_ref=xr.at[me],
            send_sem=x_send,
            recv_sem=x_recv,
            device_id=device,
            device_id_type=MESH,
        ).start()

    each_peer(send_x)
    xr[me] = nb[me_a]

    def wait_all(buffer, sem):
        block = buffer.at[pl.ds(0, total - 1)]
        pltpu.make_async_copy(block, block, sem).wait()

    wait_all(xr, x_recv)
    tiles = x32.shape[0]
    per_tile = x32.shape[1] // here

    def unpack(t, carry):
        for j in range(per_tile):
            x32[t, j * here : (j + 1) * here, :] = xr[t * per_tile + j].astype(F32)
        return carry

    lax.fori_loop(0, tiles, unpack, 0, unroll=min(8, tiles))
    every_row = x32[...].reshape(rows, part).astype(BF16)
    picked = jnp.dot(hot, every_row, preferred_element_type=F32).astype(BF16)

    sends = []

    def push(src_ref, dst_ref, send_sem, recv_sem, device):
        copy = pltpu.make_async_remote_copy(
            src_ref=src_ref,
            dst_ref=dst_ref,
            send_sem=send_sem,
            recv_sem=recv_sem,
            device_id=device,
            device_id_type=MESH,
        )
        copy.start()
        sends.append(copy)
        return copy

    def across(shift):
        return {"attn": side_of(shift, 1), "expert": me_e, "loop": me_l}

    def gate_up(shift, side, cut):
        k, pair = w_copies[shift, side, cut]
        for copy in pair:
            copy.wait()
        gate = jnp.dot(picked, wg[k], preferred_element_type=F32)
        up = jnp.dot(picked, wu[k], preferred_element_type=F32)
        return jnp.concatenate([gate, up], axis=0)

    def to_partner(shift):
        copies = []
        for cut in range(cuts):
            k = shift * cuts + cut
            ps[k] = gate_up(shift, 0, cut).astype(BF16)
            copies.append(push(ps.at[k], pr.at[k], p_send.at[k], p_recv.at[k], partner))
        return copies

    crossing = {}
    for shift in range(1, chips):
        near = to_partner(shift)
        for cut in range(cuts):
            k = (shift - 1) * cuts + cut
            both = gate_up(shift, 1, cut)
            near[cut].wait_recv()
            cs[k] = (both + pr[shift * cuts + cut].astype(F32)).astype(BF16)
            crossing[shift, cut] = push(
                cs.at[k], cr.at[k], c_send.at[k], c_recv.at[k], across(shift)
            )
    near = to_partner(0)
    for cut in range(cuts):
        own[cut] = gate_up(0, 1, cut)

    def down(k):
        d_copies[k].wait()
        return jnp.dot(hid[k], wd[k], preferred_element_type=F32)

    def spread(shift, cut):
        k = 2 * shift * cuts + cut
        return push(hid.at[k], hid.at[k + cuts], f_send.at[shift * cuts + cut],
                    f_recv.at[shift * cuts + cut], partner)

    expert_out = jnp.zeros((cap, part), F32)
    far, beside = {}, {}
    for cut in range(cuts):
        near[cut].wait_recv()
        both = own[cut] + pr[cut].astype(F32)
        for shift in range(1, chips):
            crossing[shift, cut].wait_recv()
            both = both + cr[(shift - 1) * cuts + cut].astype(F32)
        gate = both[:cap]
        hid[cut] = (gate / (1.0 + jnp.exp(-gate)) * both[cap:]).astype(BF16)
        for shift in range(1, chips):
            k = shift * cuts + cut
            far[shift, cut] = push(
                hid.at[cut], hid.at[2 * shift * cuts + cut], h_send.at[k], h_recv.at[k], across(shift)
            )
        beside[0, cut] = spread(0, cut)
        expert_out = expert_out + down(cut)
    for cut in range(cuts):
        beside[0, cut].wait_recv()
        expert_out = expert_out + down(cuts + cut)
    for shift in range(1, chips):
        for cut in range(cuts):
            far[shift, cut].wait_recv()
            beside[shift, cut] = spread(shift, cut)
            expert_out = expert_out + down(2 * shift * cuts + cut)
    for shift in range(1, chips):
        for cut in range(cuts):
            beside[shift, cut].wait_recv()
            expert_out = expert_out + down((2 * shift + 1) * cuts + cut)

    if slots > cap:
        expert_out = jnp.concatenate([expert_out, jnp.zeros((slots - cap, part), F32)], axis=0)
    high = expert_out.astype(BF16)
    low = (expert_out - high.astype(F32)).astype(BF16)
    dense = (
        jnp.dot(hot_t, high, preferred_element_type=F32)
        + jnp.dot(hot_t, low, preferred_element_type=F32)
    ) * row_weight
    d32[...] = dense.reshape(d32.shape)

    def pack(t, carry):
        for j in range(per_tile):
            ys[t * per_tile + j] = d32[t, j * here : (j + 1) * here, :].astype(BF16)
        return carry

    lax.fori_loop(0, tiles, pack, 0, unroll=min(8, tiles))

    def send_y(index, lane, device):
        pltpu.make_async_remote_copy(
            src_ref=ys.at[index],
            dst_ref=yr.at[me],
            send_sem=y_send,
            recv_sem=y_recv,
            device_id=device,
            device_id_type=MESH,
        ).start()

    for lane in range(2):

        @pl.when(me != lane)
        def _():
            send_y(lane, lane, {"attn": lane, "expert": 0, "loop": 0})

    def send_rest(index, lane, device):
        @pl.when(index > 1)
        def _():
            send_y(index, lane, device)

    each_peer(send_rest)
    yr[me] = ys[me]
    wait_all(yr, y_recv)
    def add(g, sums):
        return tuple(sums[a] + yr[g * n + a].astype(F32) for a in range(n))

    sums = lax.fori_loop(
        0,
        sources,
        add,
        tuple(jnp.zeros((here, part), F32) for _ in range(n)),
        unroll=min(8, sources),
    )
    moe = jnp.concatenate(sums, axis=1).astype(BF16).astype(F32)
    out_ref[...] = (residual + moe).astype(BF16)

    for copy in sends:
        copy.wait_send()
    wait_all(xr, x_send)
    wait_all(yr, y_send)


def per_device(
    n,
    experts,
    loops,
    resid,
    query,
    key_cache,
    value_cache,
    new_key,
    new_value,
    cache_len,
    norm_gain,
    gate_weight,
    up_weight,
    down_weight,
    block_rows,
    slot_weight,
):
    here, width = resid.shape
    total = n * experts * loops
    chips = n // 2
    rows = here * total
    part = width // n
    quarter = gate_weight.shape[2] // n
    cuts = CUTS if quarter % (128 * CUTS) == 0 else 1
    piece = quarter // cuts
    slots = block_rows.shape[1] * block_rows.shape[2]
    busiest = rows // 2
    shared = -(-(2 * rows - busiest) // (experts - 1))
    cap = min(slots, rows, (max(busiest, shared) // 8 + 1) * 8)
    cache, kv_width = key_cache.shape[1:]
    dma = pltpu.SemaphoreType.DMA
    vmem = pl.BlockSpec(memory_space=pltpu.VMEM)
    hbm = pl.BlockSpec(memory_space=pl.ANY)
    smem = pltpu.SMEM
    scratch = [
        smem((here,), jnp.int32),
        pltpu.VMEM((here, width), BF16),
        pltpu.VMEM((here, width), BF16),
        pltpu.VMEM((here, kv_width), BF16),
        pltpu.VMEM((here, kv_width), BF16),
        pltpu.VMEM((1, width), F32),
        pltpu.VMEM((1, slots), jnp.int32),
        pltpu.VMEM((1, slots), F32),
        dma((8,)),
        pltpu.VMEM((here, cache, kv_width), BF16),
        pltpu.VMEM((here, cache, kv_width), BF16),
        pltpu.VMEM((n * cuts, part, piece), BF16),
        pltpu.VMEM((n * cuts, part, piece), BF16),
        pltpu.VMEM((n * cuts, piece, part), BF16),
        pltpu.VMEM((n, here, part), BF16),
        pltpu.VMEM((total, here, part), BF16),
        pltpu.VMEM((rows // 8, 8, part), F32),
        pltpu.VMEM((chips * cuts, 2 * cap, piece), BF16),
        pltpu.VMEM((chips * cuts, 2 * cap, piece), BF16),
        pltpu.VMEM((cuts, 2 * cap, piece), F32),
        pltpu.VMEM(((chips - 1) * cuts, 2 * cap, piece), BF16),
        pltpu.VMEM(((chips - 1) * cuts, 2 * cap, piece), BF16),
        pltpu.VMEM((n * cuts, cap, piece), BF16),
        pltpu.VMEM((rows // 8, 8, part), F32),
        pltpu.VMEM((total, here, part), BF16),
        pltpu.VMEM((total, here, part), BF16),
        dma((2, here)),
        dma((2, n * cuts)),
        dma((n * cuts,)),
        dma,
        dma,
        dma((chips * cuts,)),
        dma((chips * cuts,)),
        dma(((chips - 1) * cuts,)),
        dma(((chips - 1) * cuts,)),
        dma((chips * cuts,)),
        dma((chips * cuts,)),
        dma((chips * cuts,)),
        dma((chips * cuts,)),
        dma,
        dma,
    ]
    return pl.pallas_call(
        functools.partial(kernel, (n, experts, loops, cap, cuts)),
        out_shape=pltpu.VMEM((here, width), BF16),
        in_specs=[hbm] * 13,
        out_specs=vmem,
        scratch_shapes=scratch,
        compiler_params=pltpu.CompilerParams(
            collective_id=0, has_side_effects=True, vmem_limit_bytes=VMEM_LIMIT
        ),
        name="moe_decode",
    )(
        cache_len,
        resid,
        query,
        new_key,
        new_value,
        norm_gain.reshape(1, width),
        block_rows.reshape(1, slots),
        slot_weight.reshape(1, slots),
        key_cache,
        value_cache,
        gate_weight,
        up_weight,
        down_weight,
    )


def solution(mesh):
    in_specs = (
        P(("expert", "loop", "attn"), None),
        P(("expert", "loop", "attn"), None),
        P(("expert", "loop", "attn"), None, None),
        P(("expert", "loop", "attn"), None, None),
        P(("expert", "loop", "attn"), None),
        P(("expert", "loop", "attn"), None),
        P(("expert", "loop", "attn")),
        P(),
        P("expert", "attn", "loop"),
        P("expert", "attn", "loop"),
        P("expert", "loop", "attn"),
        P("expert", None, None),
        P("expert", None, None),
    )
    out_specs = P(("expert", "loop", "attn"), None)
    body = functools.partial(
        per_device, mesh.shape["attn"], mesh.shape["expert"], mesh.shape["loop"]
    )
    return jax.shard_map(body, mesh=mesh, in_specs=in_specs, out_specs=out_specs, check_vma=False)
```

```python
import functools

import jax
import jax.numpy as jnp
from jax import lax
from jax.experimental import pallas as pl
from jax.experimental.pallas import tpu as pltpu
from jax.sharding import PartitionSpec as P

Q_HEADS = 24
KV_HEADS = 4
HEAD = 128
MESH = pl.DeviceIdType.MESH
F32 = jnp.float32
BF16 = jnp.bfloat16
VMEM_LIMIT = 56 << 20
KEPT = 2
RAW = 1
STRAIGHT = 0
AHEAD = 2


def kernel(
    sizes,
    len_hbm,
    resid_hbm,
    query_hbm,
    nk_hbm,
    nv_hbm,
    gain_hbm,
    list_hbm,
    slotw_hbm,
    kc_hbm,
    vc_hbm,
    wg_hbm,
    wu_hbm,
    wd_hbm,
    out_ref,
    len_ref,
    resid_ref,
    query_ref,
    nk_ref,
    nv_ref,
    gain_ref,
    list_ref,
    slotw_ref,
    in_sem,
    kc,
    vc,
    wg,
    wu,
    wd,
    nb,
    xr,
    x32,
    ps,
    pr,
    own,
    cs,
    cr,
    hid,
    d32,
    ys,
    yr,
    kv_sem,
    w_sem,
    sent,
    x_recv,
    p_recv,
    c_recv,
    h_recv,
    f_recv,
    y_recv,
):
    n, experts, loops, cap, live, piece, kept, wide, raw, straight = sizes
    total = n * experts * loops
    chips = n // 2
    here, width = resid_ref.shape
    cache = kc.shape[1]
    part = width // n
    rows = total * here
    others = chips - 1
    slots = list_ref.shape[1]
    me_a = lax.axis_index("attn")
    me_e = lax.axis_index("expert")
    me_l = lax.axis_index("loop")
    me = (me_e * loops + me_l) * n + me_a
    core = lax.rem(me_a, 2)
    chip = lax.div(me_a, 2)
    partner = {"attn": chip * 2 + 1 - core, "expert": me_e, "loop": me_l}

    sources = total // n
    group = me_e * loops + me_l
    lanes_of = [lax.rem(me_a + d, n) for d in range(n)]

    def peers_of(d, first, act):
        other = group ^ d if sources & (sources - 1) == 0 else lax.rem(group + d, sources)
        expert = lax.div(other, loops)
        loop = lax.rem(other, loops)
        for k in range(first, n):
            act(
                other * n + lanes_of[k],
                lanes_of[k],
                {"attn": lanes_of[k], "expert": expert, "loop": loop},
            )

    def each_peer(act):
        def step(d, carry):
            peers_of(sources - d, 0, act)
            return carry

        lax.fori_loop(1, sources, step, 0, unroll=sources <= 8)
        peers_of(0, 1, act)

    def side_of(shift, side):
        at = lax.rem(chip + shift + chips, chips)
        return at * 2 + (core if side else 1 - core)

    barrier = pltpu.get_barrier_semaphore()

    def greet(index, lane, device):
        pl.semaphore_signal(barrier, inc=1, device_id=device, device_id_type=MESH)

    in_copies = [
        pltpu.make_async_copy(source, target, in_sem)
        for source, target in (
            (query_hbm, query_ref),
            (nk_hbm, nk_ref),
            (nv_hbm, nv_ref),
            (len_hbm, len_ref),
            (resid_hbm, resid_ref),
            (gain_hbm, gain_ref),
            (list_hbm, list_ref),
            (slotw_hbm, slotw_ref),
        )
    ]
    k_copy = pltpu.make_async_copy(kc_hbm, kc, kv_sem.at[0])
    v_copy = pltpu.make_async_copy(vc_hbm, vc, kv_sem.at[1])
    g_copy = pltpu.make_async_copy(wg_hbm.at[0], wg, w_sem.at[0])
    u_copy = pltpu.make_async_copy(wu_hbm.at[0], wu, w_sem.at[1])
    d_copy = pltpu.make_async_copy(wd_hbm.at[0], wd, w_sem.at[2])
    for copy in in_copies[:4] + [k_copy] + in_copies[4:] + [v_copy]:
        copy.start()
    each_peer(greet)
    for copy in (g_copy, u_copy, d_copy):
        copy.start()

    groups = Q_HEADS // KV_HEADS
    scale = HEAD ** (-0.5)
    heads = here * Q_HEADS
    for copy in in_copies:
        copy.wait()
    head_of = lax.rem(lax.broadcasted_iota(jnp.int32, (heads, HEAD), 0), Q_HEADS) // groups
    row_of = lax.broadcasted_iota(jnp.int32, (heads, cache), 0) // Q_HEADS
    position = lax.broadcasted_iota(jnp.int32, (heads, cache), 1)
    length = len_ref[0]
    for r in range(1, here):
        length = jnp.where(row_of >= r, len_ref[r], length)
    queries = query_ref[...].astype(F32)
    new_keys = nk_ref[...].astype(F32)
    new_values = nv_ref[...].astype(F32)
    q_all = jnp.concatenate(
        [
            queries[r : r + 1, j * HEAD : (j + 1) * HEAD]
            for r in range(here)
            for j in range(Q_HEADS)
        ],
        axis=0,
    )

    def own_rows(new):
        return jnp.concatenate(
            [
                jnp.broadcast_to(new[r : r + 1, g * HEAD : (g + 1) * HEAD], (groups, HEAD))
                for r in range(here)
                for g in range(KV_HEADS)
            ],
            axis=0,
        )

    own_key, own_value = own_rows(new_keys), own_rows(new_values)
    q_wide = jnp.concatenate(
        [jnp.where(head_of == g, q_all, 0.0) for g in range(KV_HEADS)], axis=1
    ).astype(BF16)
    own_score = jnp.sum(q_all * own_key, axis=1, keepdims=True) * scale

    k_copy.wait()
    scores = jnp.concatenate(
        [
            lax.dot_general(
                q_wide[r * Q_HEADS : (r + 1) * Q_HEADS],
                kc[r],
                (((1,), (1,)), ((), ())),
                preferred_element_type=F32,
            )
            for r in range(here)
        ],
        axis=0,
    )
    scores = jnp.where(position < length, scores * scale, -jnp.inf)
    top = jnp.maximum(jnp.max(scores, axis=1, keepdims=True), own_score)
    exps = jnp.exp(scores - top)
    own_exp = jnp.exp(own_score - top)
    denominator = jnp.sum(exps, axis=1, keepdims=True) + own_exp
    probs = (exps / denominator).astype(BF16)
    own_prob = (own_exp / denominator).astype(BF16).astype(F32)
    v_copy.wait()
    mixed = jnp.concatenate(
        [
            jnp.dot(
                probs[r * Q_HEADS : (r + 1) * Q_HEADS], vc[r], preferred_element_type=F32
            )
            for r in range(here)
        ],
        axis=0,
    )
    attended = own_prob * own_value
    for g in range(KV_HEADS):
        attended = attended + jnp.where(
            head_of == g, mixed[:, g * HEAD : (g + 1) * HEAD], 0.0
        )
    attended = jnp.concatenate(
        [
            jnp.concatenate(
                [attended[r * Q_HEADS + j : r * Q_HEADS + j + 1, :] for j in range(Q_HEADS)],
                axis=1,
            )
            for r in range(here)
        ],
        axis=0,
    )
    residual = (resid_ref[...].astype(F32) + attended).astype(BF16).astype(F32)
    normed = (
        residual
        * lax.rsqrt(jnp.mean(residual * residual, axis=-1, keepdims=True) + 1e-05)
        * gain_ref[...]
    ).astype(BF16)
    for a in range(n):
        nb[a] = normed[:, a * part : (a + 1) * part]

    pl.semaphore_wait(barrier, total - 1)

    def send_x(index, lane, device):
        pltpu.make_async_remote_copy(
            src_ref=nb.at[lane],
            dst_ref=xr.at[me],
            send_sem=sent,
            recv_sem=x_recv,
            device_id=device,
            device_id_type=MESH,
        ).start()

    each_peer(send_x)
    xr[me] = nb[me_a]

    rows_pad = max(rows, 128)
    slot_rows = list_ref[...]
    hot_t = jnp.where(
        lax.broadcasted_iota(jnp.int32, (rows_pad, slots), 0) == slot_rows, 1.0, 0.0
    ).astype(F32)
    hot = hot_t.T[:cap, :rows].astype(BF16)
    hot_t = hot_t[:rows]
    row_weight = jnp.sum(hot_t * slotw_ref[...], axis=1, keepdims=True)
    hot_t = hot_t.astype(BF16)


    def wait_all(buffer, sem):
        block = buffer.at[pl.ds(0, total - 1)]
        pltpu.make_async_copy(block, block, sem).wait()

    wait_all(xr, x_recv)
    tiles = x32.shape[0]
    per_tile = x32.shape[1] // here

    def unpack(t, carry):
        for j in range(per_tile):
            x32[t, j * here : (j + 1) * here, :] = xr[t * per_tile + j].astype(F32)
        return carry

    lax.fori_loop(0, tiles, unpack, 0, unroll=min(8, tiles))
    every_row = x32[...].reshape(rows, part).astype(BF16)
    picked = jnp.dot(hot, every_row, preferred_element_type=F32).astype(BF16)

    def push(src_ref, dst_ref, recv_sem, device):
        copy = pltpu.make_async_remote_copy(
            src_ref=src_ref,
            dst_ref=dst_ref,
            send_sem=sent,
            recv_sem=recv_sem,
            device_id=device,
            device_id_type=MESH,
        )
        copy.start()
        return copy

    def across(shift):
        return {"attn": side_of(shift, 1), "expert": me_e, "loop": me_l}

    def kept_at(lane, j):
        return pl.multiple_of((lane * kept + j) * piece, piece)

    def wide_at(which, j):
        return pl.multiple_of((n * kept + which * wide + j) * piece, piece)

    g_copy.wait()
    u_copy.wait()

    def gate_up(at):
        columns = pl.ds(at, piece)
        gate = jnp.dot(picked, wg[:, columns], preferred_element_type=F32)
        up = jnp.dot(picked, wu[:, columns], preferred_element_type=F32)
        return jnp.concatenate([gate[:live], up[:live]], axis=0)

    near = {}

    def to_partner(name, at):
        k = len(near)
        ps[k] = gate_up(at).astype(BF16)
        near[name] = (k, push(ps.at[k], pr.at[k], p_recv.at[k], partner))

    def chip_sum(name, at):
        both = gate_up(at)
        k, copy = near[name]
        copy.wait_recv()
        return both + pr[k].astype(F32)

    crossing = {}

    def cross_kept(shift, j):
        k = (shift - 1) * kept + j
        cs[k] = chip_sum(("x", shift, j), kept_at(side_of(shift, 1), j)).astype(BF16)
        crossing["x", shift, j] = (k, push(cs.at[k], cr.at[k], c_recv.at[k], across(shift)))

    def cross_raw(shift, side, j):
        own_core = (shift - 1) * kept + j
        other_core = others * (kept + wide) + (shift - 1) * raw + j
        k = own_core if side else others * kept + wide + (shift - 1) * raw + j
        at = own_core if side else other_core
        lane = side_of(shift, side)
        cs[k] = gate_up(kept_at(lane, j)).astype(BF16)
        crossing["x" if side else "r", shift, j] = (
            at,
            push(
                cs.at[k],
                cr.at[at],
                c_recv.at[at],
                {"attn": lane, "expert": me_e, "loop": me_l},
            ),
        )

    def cross_wide(j):
        k = others * kept + j
        both = chip_sum(("f", j), wide_at(core, j))
        own[kept + j] = both
        cs[k] = both.astype(BF16)
        for shift in range(1, chips):
            at = others * kept + (shift - 1) * wide + j
            crossing["f", shift, j] = (
                at,
                push(cs.at[k], cr.at[at], c_recv.at[at], across(shift)),
            )

    def near_wide(j):
        to_partner(("f", j), wide_at(1 - core, j))

    ahead = min(AHEAD, wide)
    for shift in range(1, chips):
        for j in range(raw):
            cross_raw(shift, 1, j)
            cross_raw(shift, 0, j)
    for shift in range(1, chips):
        for j in range(raw, kept):
            to_partner(("x", shift, j), kept_at(side_of(shift, 0), j))
    for j in range(ahead):
        near_wide(j)
    for shift in range(1, chips):
        for j in range(raw, kept):
            cross_kept(shift, j)
    for j in range(wide):
        cross_wide(j)
        if j + ahead < wide:
            near_wide(j + ahead)
    for j in range(kept):
        to_partner(("o", j), kept_at(side_of(0, 0), j))
    for j in range(kept):
        own[j] = gate_up(kept_at(me_a, j))

    d_copy.wait()

    def down(k, at):
        return jnp.dot(hid[k], wd[pl.ds(at, piece), :], preferred_element_type=F32)

    first_wide = n * kept
    spreads = {}

    def spread(k, step):
        f = len(spreads)
        spreads[k] = push(hid.at[k], hid.at[k + step], f_recv.at[f], partner)

    crossed_raw = [("x", j) for j in range(raw)]

    def gather(kind, j, both):
        for shift in range(1, chips):
            k, copy = crossing[kind, shift, j]
            copy.wait_recv()
            both = both + cr[k].astype(F32)
            if (kind, j) in crossed_raw:
                k, copy = crossing["r", shift, j]
                copy.wait_recv()
                both = both + cr[k].astype(F32)
        gate = both[:live]
        hidden = gate / (1.0 + jnp.exp(-gate)) * both[live:]
        if cap > live:
            hidden = jnp.concatenate([hidden, jnp.zeros((cap - live, piece), F32)], axis=0)
        return hidden.astype(BF16)

    far = {}

    def kept_hidden(j):
        k, copy = near["o", j]
        copy.wait_recv()
        hid[j] = gather("x", j, own[j] + pr[k].astype(F32))
        for shift in range(1, chips):
            h = (shift - 1) * kept + j
            far[shift, j] = push(
                hid.at[j], hid.at[2 * shift * kept + j], h_recv.at[h], across(shift)
            )
        spread(j, kept)
        if j >= kept - straight:
            for shift in range(1, chips):
                k = 2 * shift * kept + kept + j
                f = len(spreads)
                spreads[2 * shift * kept + j] = push(
                    hid.at[j],
                    hid.at[k],
                    f_recv.at[f],
                    {"attn": side_of(shift, 0), "expert": me_e, "loop": me_l},
                )
        return down(j, kept_at(me_a, j))

    def wide_hidden(j):
        k = first_wide + j
        hid[k] = gather("f", j, own[kept + j])
        spread(k, wide)
        return down(k, wide_at(core, j))

    def far_hidden(shift, j):
        k = 2 * shift * kept + j
        far[shift, j].wait_recv()
        if j < kept - straight:
            spread(k, kept)
        return down(k, kept_at(side_of(-shift, 1), j))

    def beside(k, step, at):
        spreads[k].wait_recv()
        return down(k + step, at)

    def beside_kept(shift, j):
        return beside(2 * shift * kept + j, kept, kept_at(side_of(-shift, 0), j))

    def beside_wide(j):
        return beside(first_wide + j, wide, wide_at(1 - core, j))

    half = wide // 2
    steps = [(kept_hidden, j) for j in range(kept)]
    steps += [(wide_hidden, j) for j in range(half)]
    steps += [(beside_kept, 0, j) for j in range(kept)]
    steps += [(wide_hidden, j) for j in range(half, wide)]
    steps += [(beside_wide, j) for j in range(half)]
    steps += [(far_hidden, shift, j) for shift in range(1, chips) for j in range(kept)]
    steps += [(beside_wide, j) for j in range(half, wide)]
    steps += [(beside_kept, shift, j) for shift in range(1, chips) for j in range(kept)]
    expert_out = jnp.zeros((cap, part), F32)
    for step, *at in steps:
        expert_out = expert_out + step(*at)

    if slots > cap:
        expert_out = jnp.concatenate([expert_out, jnp.zeros((slots - cap, part), F32)], axis=0)
    dense = jnp.dot(hot_t, expert_out.astype(BF16), preferred_element_type=F32) * row_weight
    d32[...] = dense.reshape(d32.shape)

    def pack(t, carry):
        for j in range(per_tile):
            ys[t * per_tile + j] = d32[t, j * here : (j + 1) * here, :].astype(BF16)
        return carry

    lax.fori_loop(0, tiles, pack, 0, unroll=min(8, tiles))

    def send_y(index, lane, device):
        pltpu.make_async_remote_copy(
            src_ref=ys.at[index],
            dst_ref=yr.at[me],
            send_sem=sent,
            recv_sem=y_recv,
            device_id=device,
            device_id_type=MESH,
        ).start()

    def send_group(t, carry):
        for lane in range(n):
            index = t * n + lane

            @pl.when(index != me)
            def _():
                send_y(
                    index,
                    lane,
                    {"attn": lane, "expert": lax.div(t, loops), "loop": lax.rem(t, loops)},
                )

        return carry

    lax.fori_loop(0, sources, send_group, 0, unroll=sources <= 8)
    yr[me] = ys[me]
    wait_all(yr, y_recv)

    def add(g, sums):
        return tuple(sums[a] + yr[g * n + a].astype(F32) for a in range(n))

    sums = lax.fori_loop(
        0,
        sources,
        add,
        tuple(jnp.zeros((here, part), F32) for _ in range(n)),
        unroll=min(8, sources),
    )
    moe = jnp.concatenate(sums, axis=1).astype(BF16).astype(F32)
    out_ref[...] = (residual + moe).astype(BF16)

    def wait_sent(block):
        pltpu.make_async_copy(block, block, sent).wait()

    wait_all(xr, sent)
    wait_all(yr, sent)
    wait_sent(ps)
    wait_sent(cs.at[pl.ds(0, others * kept)])
    if raw:
        wait_sent(cs.at[pl.ds(others * kept + wide, others * raw)])
    for _ in range(others):
        if wide:
            wait_sent(cs.at[pl.ds(others * kept, wide)])
        wait_sent(hid.at[pl.ds(0, kept)])
    wait_sent(hid.at[pl.ds(0, chips * kept + wide)])


def per_device(
    n,
    experts,
    loops,
    resid,
    query,
    key_cache,
    value_cache,
    new_key,
    new_value,
    cache_len,
    norm_gain,
    gate_weight,
    up_weight,
    down_weight,
    block_rows,
    slot_weight,
):
    here, width = resid.shape
    total = n * experts * loops
    chips = n // 2
    rows = here * total
    part = width // n
    units = gate_weight.shape[2]
    piece = 256 if units % (256 * n) == 0 else 128
    pieces = units // piece
    kept = min(KEPT, pieces // n)
    wide = (pieces - n * kept) // 2
    others = chips - 1
    slots = block_rows.shape[1] * block_rows.shape[2]
    busiest = rows // 2
    shared = -(-(2 * rows - busiest) // (experts - 1))
    cap = min(slots, rows, (max(busiest, shared) // 8 + 1) * 8)
    raw = RAW if wide else 0
    straight = STRAIGHT if wide else 0
    live = min(cap, (max(busiest, shared) // 4 + 1) * 4)
    cache, kv_width = key_cache.shape[1:]
    dma = pltpu.SemaphoreType.DMA
    vmem = pl.BlockSpec(memory_space=pltpu.VMEM)
    hbm = pl.BlockSpec(memory_space=pl.ANY)
    scratch = [
        pltpu.SMEM((here,), jnp.int32),
        pltpu.VMEM((here, width), BF16),
        pltpu.VMEM((here, width), BF16),
        pltpu.VMEM((here, kv_width), BF16),
        pltpu.VMEM((here, kv_width), BF16),
        pltpu.VMEM((1, width), F32),
        pltpu.VMEM((1, slots), jnp.int32),
        pltpu.VMEM((1, slots), F32),
        dma,
        pltpu.VMEM((here, cache, kv_width), BF16),
        pltpu.VMEM((here, cache, kv_width), BF16),
        pltpu.VMEM((part, units), BF16),
        pltpu.VMEM((part, units), BF16),
        pltpu.VMEM((units, part), BF16),
        pltpu.VMEM((n, here, part), BF16),
        pltpu.VMEM((total, here, part), BF16),
        pltpu.VMEM((rows // 8, 8, part), F32),
        pltpu.VMEM((chips * kept + wide - others * raw, 2 * live, piece), BF16),
        pltpu.VMEM((chips * kept + wide - others * raw, 2 * live, piece), BF16),
        pltpu.VMEM((kept + wide, 2 * live, piece), F32),
        pltpu.VMEM((others * (kept + raw) + wide, 2 * live, piece), BF16),
        pltpu.VMEM((others * (kept + wide + raw), 2 * live, piece), BF16),
        pltpu.VMEM((pieces, cap, piece), BF16),
        pltpu.VMEM((rows // 8, 8, part), F32),
        pltpu.VMEM((total, here, part), BF16),
        pltpu.VMEM((total, here, part), BF16),
        dma((2,)),
        dma((3,)),
        dma,
        dma,
        dma((chips * kept + wide - others * raw,)),
        dma((others * (kept + wide + raw),)),
        dma((others * kept,)),
        dma((chips * kept + wide,)),
        dma,
    ]
    return pl.pallas_call(
        functools.partial(kernel, (n, experts, loops, cap, live, piece, kept, wide, raw, straight)),
        out_shape=pltpu.VMEM((here, width), BF16),
        in_specs=[hbm] * 13,
        out_specs=vmem,
        scratch_shapes=scratch,
        compiler_params=pltpu.CompilerParams(
            collective_id=0, has_side_effects=True, vmem_limit_bytes=VMEM_LIMIT
        ),
        name="moe_decode",
    )(
        cache_len,
        resid,
        query,
        new_key,
        new_value,
        norm_gain.reshape(1, width),
        block_rows.reshape(1, slots),
        slot_weight.reshape(1, slots),
        key_cache,
        value_cache,
        gate_weight,
        up_weight,
        down_weight,
    )


def solution(mesh):
    in_specs = (
        P(("expert", "loop", "attn"), None),
        P(("expert", "loop", "attn"), None),
        P(("expert", "loop", "attn"), None, None),
        P(("expert", "loop", "attn"), None, None),
        P(("expert", "loop", "attn"), None),
        P(("expert", "loop", "attn"), None),
        P(("expert", "loop", "attn")),
        P(),
        P("expert", "attn", "loop"),
        P("expert", "attn", "loop"),
        P("expert", "loop", "attn"),
        P("expert", None, None),
        P("expert", None, None),
    )
    out_specs = P(("expert", "loop", "attn"), None)
    body = functools.partial(
        per_device, mesh.shape["attn"], mesh.shape["expert"], mesh.shape["loop"]
    )
    return jax.shard_map(body, mesh=mesh, in_specs=in_specs, out_specs=out_specs, check_vma=False)
```

```python
import functools

import jax
import jax.numpy as jnp
from jax import lax
from jax.experimental import pallas as pl
from jax.experimental.pallas import tpu as pltpu
from jax.sharding import PartitionSpec as P

Q_HEADS = 24
KV_HEADS = 4
HEAD = 128
MESH = pl.DeviceIdType.MESH
F32 = jnp.float32
BF16 = jnp.bfloat16
VMEM_LIMIT = 56 << 20
KEPT = 3
RAW = 1
STRAIGHT = 2


def kernel(
    sizes,
    len_hbm,
    resid_hbm,
    query_hbm,
    nk_hbm,
    nv_hbm,
    gain_hbm,
    list_hbm,
    slotw_hbm,
    kc_hbm,
    vc_hbm,
    wg_hbm,
    wu_hbm,
    wd_hbm,
    out_ref,
    len_ref,
    resid_ref,
    query_ref,
    nk_ref,
    nv_ref,
    gain_ref,
    list_ref,
    slotw_ref,
    in_sem,
    kc,
    vc,
    wg,
    wu,
    wd,
    nb,
    xr,
    x32,
    ps,
    pr,
    own,
    cs,
    cr,
    hid,
    d32,
    ys,
    yr,
    kv_sem,
    w_sem,
    sent,
    x_recv,
    p_recv,
    c_recv,
    h_recv,
    f_recv,
    y_recv,
):
    n, experts, loops, cap, live, piece, kept, wide, raw, straight = sizes
    total = n * experts * loops
    chips = n // 2
    here, width = resid_ref.shape
    cache = kc.shape[1]
    part = width // n
    rows = total * here
    others = chips - 1
    slots = list_ref.shape[1]
    me_a = lax.axis_index("attn")
    me_e = lax.axis_index("expert")
    me_l = lax.axis_index("loop")
    me = (me_e * loops + me_l) * n + me_a
    core = lax.rem(me_a, 2)
    chip = lax.div(me_a, 2)
    partner = {"attn": chip * 2 + 1 - core, "expert": me_e, "loop": me_l}

    sources = total // n
    group = me_e * loops + me_l
    lanes_of = [lax.rem(me_a + d, n) for d in range(n)]

    def peers_of(d, first, act):
        other = group ^ d if sources & (sources - 1) == 0 else lax.rem(group + d, sources)
        expert = lax.div(other, loops)
        loop = lax.rem(other, loops)
        for k in range(first, n):
            act(
                other * n + lanes_of[k],
                lanes_of[k],
                {"attn": lanes_of[k], "expert": expert, "loop": loop},
            )

    def each_peer(act):
        def step(d, carry):
            peers_of(sources - d, 0, act)
            return carry

        lax.fori_loop(1, sources, step, 0, unroll=sources <= 8)
        peers_of(0, 1, act)

    def side_of(shift, side):
        at = lax.rem(chip + shift + chips, chips)
        return at * 2 + (core if side else 1 - core)

    barrier = pltpu.get_barrier_semaphore()

    def greet(index, lane, device):
        pl.semaphore_signal(barrier, inc=1, device_id=device, device_id_type=MESH)

    in_copies = [
        pltpu.make_async_copy(source, target, in_sem)
        for source, target in (
            (query_hbm, query_ref),
            (nk_hbm, nk_ref),
            (nv_hbm, nv_ref),
            (len_hbm, len_ref),
            (resid_hbm, resid_ref),
            (gain_hbm, gain_ref),
            (list_hbm, list_ref),
            (slotw_hbm, slotw_ref),
        )
    ]
    k_copy = pltpu.make_async_copy(kc_hbm, kc, kv_sem.at[0])
    v_copy = pltpu.make_async_copy(vc_hbm, vc, kv_sem.at[1])
    g_copy = pltpu.make_async_copy(wg_hbm.at[0], wg, w_sem.at[0])
    u_copy = pltpu.make_async_copy(wu_hbm.at[0], wu, w_sem.at[1])
    d_copy = pltpu.make_async_copy(wd_hbm.at[0], wd, w_sem.at[2])
    for copy in in_copies[:4] + [k_copy] + in_copies[4:] + [v_copy]:
        copy.start()
    each_peer(greet)
    for copy in (g_copy, u_copy, d_copy):
        copy.start()

    groups = Q_HEADS // KV_HEADS
    scale = HEAD ** (-0.5)
    heads = here * Q_HEADS
    for copy in in_copies:
        copy.wait()
    head_of = lax.rem(lax.broadcasted_iota(jnp.int32, (heads, HEAD), 0), Q_HEADS) // groups
    row_of = lax.broadcasted_iota(jnp.int32, (heads, cache), 0) // Q_HEADS
    position = lax.broadcasted_iota(jnp.int32, (heads, cache), 1)
    length = len_ref[0]
    for r in range(1, here):
        length = jnp.where(row_of >= r, len_ref[r], length)
    queries = query_ref[...].astype(F32)
    new_keys = nk_ref[...].astype(F32)
    new_values = nv_ref[...].astype(F32)
    q_all = jnp.concatenate(
        [
            queries[r : r + 1, j * HEAD : (j + 1) * HEAD]
            for r in range(here)
            for j in range(Q_HEADS)
        ],
        axis=0,
    )

    def own_rows(new):
        return jnp.concatenate(
            [
                jnp.broadcast_to(new[r : r + 1, g * HEAD : (g + 1) * HEAD], (groups, HEAD))
                for r in range(here)
                for g in range(KV_HEADS)
            ],
            axis=0,
        )

    own_key, own_value = own_rows(new_keys), own_rows(new_values)
    q_wide = jnp.concatenate(
        [jnp.where(head_of == g, q_all, 0.0) for g in range(KV_HEADS)], axis=1
    ).astype(BF16)
    own_score = jnp.sum(q_all * own_key, axis=1, keepdims=True) * scale

    k_copy.wait()
    scores = jnp.concatenate(
        [
            lax.dot_general(
                q_wide[r * Q_HEADS : (r + 1) * Q_HEADS],
                kc[r],
                (((1,), (1,)), ((), ())),
                preferred_element_type=F32,
            )
            for r in range(here)
        ],
        axis=0,
    )
    scores = jnp.where(position < length, scores * scale, -jnp.inf)
    top = jnp.maximum(jnp.max(scores, axis=1, keepdims=True), own_score)
    exps = jnp.exp(scores - top)
    own_exp = jnp.exp(own_score - top)
    denominator = jnp.sum(exps, axis=1, keepdims=True) + own_exp
    probs = (exps / denominator).astype(BF16)
    own_prob = (own_exp / denominator).astype(BF16).astype(F32)
    v_copy.wait()
    mixed = jnp.concatenate(
        [
            jnp.dot(
                probs[r * Q_HEADS : (r + 1) * Q_HEADS], vc[r], preferred_element_type=F32
            )
            for r in range(here)
        ],
        axis=0,
    )
    attended = own_prob * own_value
    for g in range(KV_HEADS):
        attended = attended + jnp.where(
            head_of == g, mixed[:, g * HEAD : (g + 1) * HEAD], 0.0
        )
    attended = jnp.concatenate(
        [
            jnp.concatenate(
                [attended[r * Q_HEADS + j : r * Q_HEADS + j + 1, :] for j in range(Q_HEADS)],
                axis=1,
            )
            for r in range(here)
        ],
        axis=0,
    )
    residual = (resid_ref[...].astype(F32) + attended).astype(BF16).astype(F32)
    normed = (
        residual
        * lax.rsqrt(jnp.mean(residual * residual, axis=-1, keepdims=True) + 1e-05)
        * gain_ref[...]
    ).astype(BF16)
    for a in range(n):
        nb[a] = normed[:, a * part : (a + 1) * part]

    pl.semaphore_wait(barrier, total - 1)

    def send_x(index, lane, device):
        pltpu.make_async_remote_copy(
            src_ref=nb.at[lane],
            dst_ref=xr.at[me],
            send_sem=sent,
            recv_sem=x_recv,
            device_id=device,
            device_id_type=MESH,
        ).start()

    def send_x_group(step, carry):
        g = sources - 1 - step
        for lane in range(n - 1, -1, -1):

            @pl.when(g * n + lane != me)
            def _():
                send_x(
                    g * n + lane,
                    lane,
                    {"attn": lane, "expert": lax.div(g, loops), "loop": lax.rem(g, loops)},
                )

        return carry

    lax.fori_loop(0, sources, send_x_group, 0, unroll=sources <= 8)
    xr[me] = nb[me_a]

    rows_pad = max(rows, 128)
    slot_rows = list_ref[...]
    hot_t = jnp.where(
        lax.broadcasted_iota(jnp.int32, (rows_pad, slots), 0) == slot_rows, 1.0, 0.0
    ).astype(F32)
    hot = hot_t.T[:cap, :rows].astype(BF16)
    hot_t = hot_t[:rows]
    row_weight = jnp.sum(hot_t * slotw_ref[...], axis=1, keepdims=True)
    hot_t = hot_t[:, :cap].astype(BF16)


    def wait_all(buffer, sem):
        block = buffer.at[pl.ds(0, total - 1)]
        pltpu.make_async_copy(block, block, sem).wait()

    wait_all(xr, x_recv)
    tiles = x32.shape[0]
    per_tile = x32.shape[1] // here

    def unpack(t, carry):
        for j in range(per_tile):
            x32[t, j * here : (j + 1) * here, :] = xr[t * per_tile + j].astype(F32)
        return carry

    lax.fori_loop(0, tiles, unpack, 0, unroll=min(8, tiles))
    every_row = x32[...].reshape(rows, part).astype(BF16)
    picked = jnp.dot(hot, every_row, preferred_element_type=F32).astype(BF16)

    def push(src_ref, dst_ref, recv_sem, device, when=None):
        copy = pltpu.make_async_remote_copy(
            src_ref=src_ref,
            dst_ref=dst_ref,
            send_sem=sent,
            recv_sem=recv_sem,
            device_id=device,
            device_id_type=MESH,
        )
        if when is None:
            copy.start()
        else:

            @pl.when(when)
            def _():
                copy.start()

        return copy

    def across(shift):
        return {"attn": side_of(shift, 1), "expert": me_e, "loop": me_l}

    def kept_at(lane, j):
        return pl.multiple_of((lane * kept + j) * piece, piece)

    def wide_at(which, j):
        return pl.multiple_of((n * kept + which * wide + j) * piece, piece)

    g_copy.wait()
    u_copy.wait()

    def gate_up(at, width=piece):
        columns = pl.ds(at, width)
        gate = jnp.dot(picked, wg[:, columns], preferred_element_type=F32)
        up = jnp.dot(picked, wu[:, columns], preferred_element_type=F32)
        return jnp.concatenate([gate[:live], up[:live]], axis=0)

    near = {}

    def to_partner(name, at):
        k = len(near)
        ps[k] = gate_up(at).astype(BF16)
        seat = k - kept if ("o", 0) in near else k
        near[name] = (k, push(ps.at[k], pr.at[k], p_recv.at[seat], partner))

    def chip_sum(name, at):
        both = gate_up(at)
        k, copy = near[name]
        copy.wait_recv()
        return both + pr[k].astype(F32)

    crossing = {}

    def cross_kept(shift, j):
        k = (shift - 1) * kept + j
        cs[k] = chip_sum(("x", shift, j), kept_at(side_of(shift, 1), j)).astype(BF16)
        crossing["x", shift, j] = (k, push(cs.at[k], cr.at[k], c_recv.at[k], across(shift)))

    def cross_raw(shift, side, j):
        own_core = (shift - 1) * kept + j
        other_core = others * (kept + wide) + (shift - 1) * raw + j
        k = own_core if side else others * kept + wide + (shift - 1) * raw + j
        at = own_core if side else other_core
        lane = side_of(shift, side)
        cs[k] = gate_up(kept_at(lane, j)).astype(BF16)
        crossing["x" if side else "r", shift, j] = (
            at,
            push(
                cs.at[k],
                cr.at[at],
                c_recv.at[at],
                {"attn": lane, "expert": me_e, "loop": me_l},
            ),
        )

    def cross_wide(j):
        k = others * kept + j
        both = chip_sum(("f", j), wide_at(core, j))
        own[kept + j] = both
        cs[k] = both.astype(BF16)
        for shift in range(1, chips):
            at = others * kept + (shift - 1) * wide + j
            crossing["f", shift, j] = (
                at,
                push(cs.at[k], cr.at[at], c_recv.at[at], across(shift)),
            )

    def near_wide(j):
        to_partner(("f", j), wide_at(1 - core, j))

    def near_own():
        k = len(near)
        both = gate_up(kept_at(side_of(0, 0), 0), kept * piece).astype(BF16)
        for j in range(kept):
            ps[k + j] = both[:, j * piece : (j + 1) * piece]
        pieces_of = pl.ds(k, kept)
        copy = push(ps.at[pieces_of], pr.at[pieces_of], p_recv.at[others * (kept - raw) + wide], partner)
        for j in range(kept):
            near["o", j] = (k + j, copy)

    def keep_own():
        both = gate_up(kept_at(me_a, 0), kept * piece)
        for j in range(kept):
            own[j] = both[:, j * piece : (j + 1) * piece]

    early = 1 if wide else 0
    for shift in range(1, chips):
        for j in range(raw):
            cross_raw(shift, 1, j)
            cross_raw(shift, 0, j)
    for shift in range(1, chips):
        for j in range(raw, kept):
            to_partner(("x", shift, j), kept_at(side_of(shift, 0), j))
    for j in range(early):
        near_wide(j)
    for shift in range(1, chips):
        for j in range(raw, kept):
            cross_kept(shift, j)
    near_own()
    for j in range(wide):
        cross_wide(j)
        if j + early < wide:
            near_wide(j + early)
        if j == 0:
            keep_own()
    if not wide:
        keep_own()

    d_copy.wait()

    def down(k, at):
        return jnp.dot(hid[k], wd[pl.ds(at, piece), :], preferred_element_type=F32)

    first_wide = n * kept
    spreads = {}

    def spread_at(k):
        if k >= first_wide:
            return kept + k - first_wide
        shift, j = divmod(k, 2 * kept)
        return j if shift == 0 else wide + shift * kept + j

    def spread(k, step, when=None):
        f = spread_at(k)
        spreads[k] = push(hid.at[k], hid.at[k + step], f_recv.at[f], partner, when)

    crossed_raw = [("x", j) for j in range(raw)]

    def gather(kind, j, both):
        for shift in range(1, chips):
            k, copy = crossing[kind, shift, j]
            copy.wait_recv()
            both = both + cr[k].astype(F32)
            if (kind, j) in crossed_raw:
                k, copy = crossing["r", shift, j]
                copy.wait_recv()
                both = both + cr[k].astype(F32)
        gate = both[:live]
        hidden = gate / (1.0 + jnp.exp(-gate)) * both[live:]
        if cap > live:
            hidden = jnp.concatenate([hidden, jnp.zeros((cap - live, piece), F32)], axis=0)
        return hidden.astype(BF16)

    far = {}

    def kept_hidden(j):
        k, copy = near["o", j]
        if j == 0:
            copy.wait_recv()
        hid[j] = gather("x", j, own[j] + pr[k].astype(F32))
        for shift in range(1, chips):
            h = (shift - 1) * kept + j
            far[shift, j] = push(
                hid.at[j], hid.at[2 * shift * kept + j], h_recv.at[h], across(shift)
            )
        spread(j, kept)
        if j >= kept - straight:
            for shift in range(1, chips):
                f = f_recv.at[spread_at(2 * shift * kept + j)]
                push(
                    hid.at[j],
                    hid.at[2 * shift * kept + kept + j],
                    f,
                    {"attn": side_of(shift, 0), "expert": me_e, "loop": me_l},
                    core == 0,
                )
        return down(j, kept_at(me_a, j))

    def wide_hidden(j):
        k = first_wide + j
        hid[k] = gather("f", j, own[kept + j])
        spread(k, wide)
        return down(k, wide_at(core, j))

    def far_hidden(shift, j):
        k = 2 * shift * kept + j
        far[shift, j].wait_recv()
        spread(k, kept, core == 1 if j >= kept - straight else None)
        return down(k, kept_at(side_of(-shift, 1), j))

    def beside(k, step, at):
        spreads[k].wait_recv()
        return down(k + step, at)

    def beside_kept(shift, j):
        return beside(2 * shift * kept + j, kept, kept_at(side_of(-shift, 0), j))

    def beside_wide(j):
        return beside(first_wide + j, wide, wide_at(1 - core, j))

    half = wide // 2
    steps = [(kept_hidden, j) for j in range(kept)]
    steps += [(beside_kept, 0, j) for j in range(kept)]
    steps += [(wide_hidden, 0)] if wide else []
    steps += [(far_hidden, shift, 0) for shift in range(1, chips)]
    steps += [(wide_hidden, j) for j in range(1, wide)]
    steps += [(beside_wide, 0)] if wide else []
    steps += [(far_hidden, shift, j) for shift in range(1, chips) for j in range(1, kept)]
    steps += [(beside_kept, shift, 0) for shift in range(1, chips)]
    steps += [(beside_wide, j) for j in range(1, wide)]
    steps += [(beside_kept, shift, j) for shift in range(1, chips) for j in range(1, kept)]
    expert_out = jnp.zeros((cap, part), F32)
    for step, *at in steps:
        expert_out = expert_out + step(*at)

    dense = jnp.dot(hot_t, expert_out.astype(BF16), preferred_element_type=F32) * row_weight
    d32[...] = dense.reshape(d32.shape)

    def send_y(index, lane, device):
        pltpu.make_async_remote_copy(
            src_ref=ys.at[index],
            dst_ref=yr.at[me],
            send_sem=sent,
            recv_sem=y_recv,
            device_id=device,
            device_id_type=MESH,
        ).start()

    def pack_group(g):
        for lane in range(n):
            row = lane * here
            tile = g * (n * here // 8) + row // 8
            ys[g * n + lane] = d32[tile, row % 8 : row % 8 + here, :].astype(BF16)

    def send_to(index, lane, device, when):
        @pl.when(when)
        def _():
            send_y(index, lane, device)

    pack_group(0)
    for lane in range(2):
        send_to(lane, lane, {"attn": lane, "expert": 0, "loop": 0}, me != lane)

    def send_lanes(g):
        for lane in range(n):
            index = g * n + lane
            send_to(
                index,
                lane,
                {"attn": lane, "expert": lax.div(g, loops), "loop": lax.rem(g, loops)},
                jnp.logical_and(index != me, index > 1),
            )

    def send_group(g, carry):
        pack_group(g)
        send_lanes(g)
        return carry

    lax.fori_loop(1, sources, send_group, 0, unroll=sources <= 8)
    send_lanes(0)
    yr[me] = ys[me]
    wait_all(yr, y_recv)

    def add(g, sums):
        return tuple(sums[a] + yr[g * n + a].astype(F32) for a in range(n))

    sums = lax.fori_loop(
        0,
        sources,
        add,
        tuple(jnp.zeros((here, part), F32) for _ in range(n)),
        unroll=min(8, sources),
    )
    moe = jnp.concatenate(sums, axis=1).astype(BF16).astype(F32)
    out_ref[...] = (residual + moe).astype(BF16)

    def wait_sent(block):
        pltpu.make_async_copy(block, block, sent).wait()

    wait_all(xr, sent)
    wait_all(yr, sent)
    wait_sent(ps)
    wait_sent(cs.at[pl.ds(0, others * kept)])
    if raw:
        wait_sent(cs.at[pl.ds(others * kept + wide, others * raw)])
    for _ in range(others):
        if wide:
            wait_sent(cs.at[pl.ds(others * kept, wide)])
        wait_sent(hid.at[pl.ds(0, kept)])
    wait_sent(hid.at[pl.ds(0, chips * kept + wide)])


def per_device(
    n,
    experts,
    loops,
    resid,
    query,
    key_cache,
    value_cache,
    new_key,
    new_value,
    cache_len,
    norm_gain,
    gate_weight,
    up_weight,
    down_weight,
    block_rows,
    slot_weight,
):
    here, width = resid.shape
    total = n * experts * loops
    chips = n // 2
    rows = here * total
    part = width // n
    units = gate_weight.shape[2]
    piece = 256 if units % (256 * n) == 0 else 128
    pieces = units // piece
    kept = min(KEPT, pieces // n)
    wide = (pieces - n * kept) // 2
    others = chips - 1
    slots = block_rows.shape[1] * block_rows.shape[2]
    busiest = rows // 2
    shared = -(-(2 * rows - busiest) // (experts - 1))
    cap = min(slots, rows, (max(busiest, shared) // 8 + 1) * 8)
    raw = RAW if wide else 0
    straight = STRAIGHT if wide else 0
    live = min(cap, (max(busiest, shared) // 4 + 1) * 4)
    cache, kv_width = key_cache.shape[1:]
    dma = pltpu.SemaphoreType.DMA
    vmem = pl.BlockSpec(memory_space=pltpu.VMEM)
    hbm = pl.BlockSpec(memory_space=pl.ANY)
    scratch = [
        pltpu.SMEM((here,), jnp.int32),
        pltpu.VMEM((here, width), BF16),
        pltpu.VMEM((here, width), BF16),
        pltpu.VMEM((here, kv_width), BF16),
        pltpu.VMEM((here, kv_width), BF16),
        pltpu.VMEM((1, width), F32),
        pltpu.VMEM((1, slots), jnp.int32),
        pltpu.VMEM((1, slots), F32),
        dma,
        pltpu.VMEM((here, cache, kv_width), BF16),
        pltpu.VMEM((here, cache, kv_width), BF16),
        pltpu.VMEM((part, units), BF16),
        pltpu.VMEM((part, units), BF16),
        pltpu.VMEM((units, part), BF16),
        pltpu.VMEM((n, here, part), BF16),
        pltpu.VMEM((total, here, part), BF16),
        pltpu.VMEM((rows // 8, 8, part), F32),
        pltpu.VMEM((chips * kept + wide - others * raw, 2 * live, piece), BF16),
        pltpu.VMEM((chips * kept + wide - others * raw, 2 * live, piece), BF16),
        pltpu.VMEM((kept + wide, 2 * live, piece), F32),
        pltpu.VMEM((others * (kept + raw) + wide, 2 * live, piece), BF16),
        pltpu.VMEM((others * (kept + wide + raw), 2 * live, piece), BF16),
        pltpu.VMEM((pieces, cap, piece), BF16),
        pltpu.VMEM((rows // 8, 8, part), F32),
        pltpu.VMEM((total, here, part), BF16),
        pltpu.VMEM((total, here, part), BF16),
        dma((2,)),
        dma((3,)),
        dma,
        dma,
        dma((chips * kept + wide - others * raw - kept + 1,)),
        dma((others * (kept + wide + raw),)),
        dma((others * kept,)),
        dma((chips * kept + wide,)),
        dma,
    ]
    return pl.pallas_call(
        functools.partial(kernel, (n, experts, loops, cap, live, piece, kept, wide, raw, straight)),
        out_shape=pltpu.VMEM((here, width), BF16),
        in_specs=[hbm] * 13,
        out_specs=vmem,
        scratch_shapes=scratch,
        compiler_params=pltpu.CompilerParams(
            collective_id=0, has_side_effects=True, vmem_limit_bytes=VMEM_LIMIT
        ),
        name="moe_decode",
    )(
        cache_len,
        resid,
        query,
        new_key,
        new_value,
        norm_gain.reshape(1, width),
        block_rows.reshape(1, slots),
        slot_weight.reshape(1, slots),
        key_cache,
        value_cache,
        gate_weight,
        up_weight,
        down_weight,
    )


def solution(mesh):
    in_specs = (
        P(("expert", "loop", "attn"), None),
        P(("expert", "loop", "attn"), None),
        P(("expert", "loop", "attn"), None, None),
        P(("expert", "loop", "attn"), None, None),
        P(("expert", "loop", "attn"), None),
        P(("expert", "loop", "attn"), None),
        P(("expert", "loop", "attn")),
        P(),
        P("expert", "attn", "loop"),
        P("expert", "attn", "loop"),
        P("expert", "loop", "attn"),
        P("expert", None, None),
        P("expert", None, None),
    )
    out_specs = P(("expert", "loop", "attn"), None)
    body = functools.partial(
        per_device, mesh.shape["attn"], mesh.shape["expert"], mesh.shape["loop"]
    )
    return jax.shard_map(body, mesh=mesh, in_specs=in_specs, out_specs=out_specs, check_vma=False)
```
